32 devices in a mesh: cols: 8 (over z, y), grp: 4 (over x, core).
Axes of the slice: x: 2, y: 2, z: 4, core: 2. Of those that a mesh axis runs over, the one named last changes fastest.
Arguments:
- hcols: float32 [8, 4, 9, 128, 128], P('cols', 'grp'), as said below
- neighbours: int32 [8, 4, 6], P('cols', 'grp'), may hold values from 0 to 8, as said below
- counts: int32 [8, 4], P('cols', 'grp'), may hold values from 4 to 6, as said below
Outputs:
- density: float32 [8, 4, 9, 128, 128], P('cols', 'grp')
The draws below stay inside these ranges and needn't reach their ends.
Inputs may be any that keep to these rules, and one draw needn't show every extreme that they name: `neighbours`: each list starts with 4 (the block column itself) and holds 6 distinct offset indices. Only the first counts entries of a list are used; some block column uses all 6. hcols describes a symmetric H as stated in the first step.
All inputs are finite; a program needn't handle non-finite values.
Results may differ from the reference program's by a relative error of at most 0.005.
Values sent between devices are 32-bit elements; how exact they have to be, the bound alone decides.
A program may use at most 64 MiB of HBM per device.

```python
import math
import jax
import jax.numpy as jnp
from jax import lax

BS = 128
NBR = 9
MAXNB = 6
MINNB = 4
N_COLS = 8
N_GRP = 4


def draw_hcols(key, part):
    key_raw, key_mag, key_sign, key_scale = jax.random.split(jax.random.fold_in(key, 11), 4)
    key_cols, key_grp, key_global, key_turn = jax.random.split(key_scale, 4)
    shape = (N_COLS, N_GRP, NBR, BS, BS)
    raw = jax.random.normal(key_raw, shape, jnp.float32)
    cols_level = jax.random.uniform(key_cols, (N_COLS,), jnp.float32, -0.15, 0.15)
    grp_level = jax.random.uniform(key_grp, (N_GRP,), jnp.float32, -0.15, 0.15)
    global_size = jax.random.uniform(key_global, (), jnp.float32, 0.2, 0.35)
    global_turn = jnp.where(jax.random.bernoulli(key_turn, 0.5), 1.0, -1.0).astype(jnp.float32)
    factor = jnp.exp(global_size * global_turn + cols_level[:, None] + grp_level[None, :])
    coupling = raw * 0.03 * factor[:, :, None, None, None]
    magnitude = jnp.exp(jax.random.uniform(key_mag, (N_COLS, N_GRP, BS), jnp.float32, math.log(0.15), math.log(1.5)))
    signs = jnp.where(jax.random.bernoulli(key_sign, 0.5, (N_COLS, N_GRP, BS)), 1.0, -1.0).astype(jnp.float32)
    position = jnp.arange(N_COLS, dtype=jnp.float32) / max(N_COLS - 1, 1)
    ramp = 0.6 + 1.2 * position
    onsite = signs * magnitude * ramp[:, None, None] * factor[:, :, None]
    identity = jnp.eye(BS, dtype=jnp.float32)
    blocks = []
    for stencil in range(9):
        if stencil < 4:
            blocks.append(coupling[:, :, stencil])
        elif stencil == 4:
            centre = coupling[:, :, 4]
            symmetric = (centre + jnp.swapaxes(centre, -1, -2)) * 0.70710678
            blocks.append(symmetric * (1.0 - identity) + identity * onsite[..., :, None])
        else:
            step_cols = stencil // 3 - 1
            step_grp = stencil % 3 - 1
            source = jnp.roll(coupling[:, :, 8 - stencil], (-step_cols, -step_grp), axis=(0, 1))
            blocks.append(jnp.swapaxes(source, -1, -2))
    return jnp.stack(blocks, axis=2).astype(jnp.float32)


def draw_neighbours(key, part):
    scores = jax.random.randint(jax.random.fold_in(key, 23), (N_COLS, N_GRP, 8), 0, 1 << 20) * 8 + jnp.arange(8, dtype=jnp.int32)
    ranking = jnp.argsort(scores, axis=-1, stable=True).astype(jnp.int32)
    offsets = jnp.where(ranking >= 4, ranking + 1, ranking)
    centre = jnp.full((N_COLS, N_GRP, 1), 4, jnp.int32)
    return jnp.concatenate([centre, offsets[..., :MAXNB - 1]], axis=-1).astype(jnp.int32)


def draw_counts(key, part):
    drawn = jax.random.randint(jax.random.fold_in(key, 37), (N_COLS, N_GRP), MINNB, MAXNB + 1).astype(jnp.int32)
    return drawn.at[0, 0].set(MAXNB).at[0, 1].set(MINNB)


def setup_inputs(seed: int = 0) -> dict:
    seeds = jax.random.split(jax.random.key(seed), 4)
    hcols = draw_hcols(jax.random.fold_in(seeds[3], 71), 0)
    neighbours = draw_neighbours(jax.random.fold_in(seeds[3], 71), 0)
    counts = draw_counts(jax.random.fold_in(seeds[3], 71), 0)
    return {"hcols": hcols, "neighbours": neighbours, "counts": counts}


exact_mode = lax.Precision.HIGHEST

def product(left, right):
    return jnp.dot(left, right, precision=exact_mode, preferred_element_type=jnp.float32)

def sign_column(matrix, spectral, block_width):
    initial = matrix / spectral
    square = product(initial, initial)
    iterate = 1.5 * initial - 0.5 * product(initial, square)
    column = iterate[:, :block_width]
    return 1.5 * column - 0.5 * product(iterate, product(iterate, column))

def assemble(beside_all, offset_ids, live_count, block_width):
    slot_count = offset_ids.shape[0]
    along_cols = offset_ids // 3 - 1
    along_grp = offset_ids % 3 - 1
    delta_cols = along_cols[:, None] - along_cols[None, :]
    delta_grp = along_grp[:, None] - along_grp[None, :]
    inside = (jnp.abs(delta_cols) <= 1) & (jnp.abs(delta_grp) <= 1)
    live_slots = jnp.arange(slot_count, dtype=jnp.int32) < live_count
    usable = inside & live_slots[:, None] & live_slots[None, :]
    stored = jnp.clip((delta_cols + 1) * 3 + (delta_grp + 1), 0, 8)
    flat_index = (offset_ids[None, :] * 9 + stored).astype(jnp.int32)
    stacked = beside_all.reshape(81, block_width, block_width)
    picked = jnp.take(stacked, flat_index.reshape(-1), axis=0)
    picked = picked.reshape(slot_count, slot_count, block_width, block_width)
    picked = jnp.where(usable[:, :, None, None], picked, jnp.float32(0.0))
    return picked.transpose(0, 2, 1, 3).reshape(slot_count * block_width, slot_count * block_width)

def scatter_out(dens_col, offset_ids, live_count, block_width):
    slot_count = offset_ids.shape[0]
    live_slots = jnp.arange(slot_count, dtype=jnp.int32) < live_count
    one_hot = ((offset_ids[:, None] == jnp.arange(9, dtype=jnp.int32)[None, :]) & live_slots[:, None]).astype(jnp.float32)
    row_blocks = dens_col.reshape(slot_count, block_width, block_width)
    return jnp.einsum('pk,pab->kab', one_hot, row_blocks, precision=exact_mode)

def reference(hcols, neighbours, counts):
    block_width = hcols.shape[-1]
    sum_squares = jnp.sum(hcols * hcols)
    spectral = 2.0 * jnp.sqrt(sum_squares / (block_width * N_COLS * N_GRP) + 1e-06)
    padded = jnp.pad(hcols, ((1, 1), (1, 1), (0, 0), (0, 0), (0, 0)), mode='wrap')
    order_full = MAXNB * block_width
    identity_cols = jnp.eye(order_full, block_width, dtype=jnp.float32)
    zero_index = jnp.zeros((), jnp.int32)

    def one_column(device_id):
        col_index = (device_id // N_GRP).astype(jnp.int32)
        grp_index = (device_id % N_GRP).astype(jnp.int32)
        beside_all = lax.dynamic_slice(padded, (col_index, grp_index, zero_index, zero_index, zero_index), (3, 3, NBR, block_width, block_width))
        offset_ids = neighbours[col_index, grp_index]
        live_count = counts[col_index, grp_index]
        matrix = assemble(beside_all, offset_ids, live_count, block_width)
        sign_col = sign_column(matrix, spectral, block_width)
        dens_col = 0.5 * (identity_cols - sign_col)
        return scatter_out(dens_col, offset_ids, live_count, block_width)
    results = lax.map(one_column, jnp.arange(N_COLS * N_GRP, dtype=jnp.int32))
    return results.reshape(hcols.shape)
```

```python
import functools

import jax
import jax.numpy as jnp
from jax import lax
from jax.experimental import pallas as pl
from jax.experimental.pallas import tpu as pltpu
from jax.sharding import PartitionSpec as P

MESH = pl.DeviceIdType.MESH
SLOTS = 6
STENCIL = 9
MISSING = 64
TURNED = 32


def transfers():
    plan = []
    for along_cols in (-1, 1):
        plan.append(((along_cols, 0), 3, 3))
    for along_cols in (-1, 1):
        for along_grp in (-1, 1):
            plan.append(((along_cols, along_grp), 4, 1))
    for along_grp, runs in ((1, ((0, 2), (4, 1), (6, 2))), (-1, ((1, 2), (4, 1), (7, 2)))):
        for first, blocks in runs:
            plan.append(((0, along_grp), first, blocks))
    placed, slot = [], STENCIL
    for offset, first, blocks in plan:
        placed.append((offset, first, blocks, slot))
        slot += blocks
    return placed, slot


def lookup(placed):
    table = [MISSING] * (STENCIL * STENCIL)
    held = [((0, 0), k, k) for k in range(STENCIL)]
    for offset, first, blocks, slot in placed:
        held += [(offset, first + i, slot + i) for i in range(blocks)]
    for (cols, grp), k, slot in held:
        row_cols, row_grp = cols + k // 3 - 1, grp + k % 3 - 1
        assert abs(row_cols) <= 1 and abs(row_grp) <= 1
        column = (cols + 1) * 3 + grp + 1
        row = (row_cols + 1) * 3 + row_grp + 1
        table[row * STENCIL + column] = slot
        if row != column:
            table[column * STENCIL + row] = slot + TURNED
    return table


def kernel(
    n_cols, n_grp, hcols, nbr, cnt, out, blk, table, high, low, dens, row_sums, col_sums,
    load_sem, send_sem, recv_sem, row_send, row_recv, col_send, col_recv,
):
    width = blk.shape[-1]
    placed, _ = transfers()
    col, grp = lax.axis_index("cols"), lax.axis_index("grp")

    def at(step_cols, step_grp):
        return (lax.rem(col + step_cols + n_cols, n_cols), lax.rem(grp + step_grp + n_grp, n_grp))

    load = pltpu.make_async_copy(hcols.at[0, 0], blk.at[pl.ds(0, STENCIL)], load_sem)
    load.start()
    barrier = pltpu.get_barrier_semaphore()

    def greet_row(i, carry):
        pl.semaphore_signal(barrier, inc=1, device_id=at(0, i), device_id_type=MESH)
        return carry

    def greet_col(i, carry):
        pl.semaphore_signal(barrier, inc=1, device_id=at(i, 0), device_id_type=MESH)
        return carry

    lax.fori_loop(1, n_grp, greet_row, 0)
    lax.fori_loop(1, n_cols, greet_col, 0)
    for step_cols in (-1, 1):
        for step_grp in (-1, 1):
            pl.semaphore_signal(
                barrier, inc=1, device_id=at(step_cols, step_grp), device_id_type=MESH
            )
    for i, value in enumerate(lookup(placed)):
        table[i] = jnp.int32(value)
    load.wait()
    own = jnp.zeros((8, width), jnp.float32)
    for k in range(STENCIL):
        part = blk[k]
        own = own + jnp.sum((part * part).reshape(width // 8, 8, width), axis=0)
    row_sums[0] = own
    pl.semaphore_wait(barrier, n_grp + n_cols + 2)

    def row_copy(i):
        return pltpu.make_async_remote_copy(
            src_ref=row_sums.at[0], dst_ref=row_sums.at[i], send_sem=row_send.at[i],
            recv_sem=row_recv.at[i], device_id=at(0, i), device_id_type=MESH,
        )

    def col_copy(i):
        return pltpu.make_async_remote_copy(
            src_ref=col_sums.at[0], dst_ref=col_sums.at[i], send_sem=col_send.at[i],
            recv_sem=col_recv.at[i], device_id=at(i, 0), device_id_type=MESH,
        )

    def start_row(i, carry):
        row_copy(i).start()
        return carry

    def start_col(i, carry):
        col_copy(i).start()
        return carry

    def wait_row(i, carry):
        row_copy(i).wait_recv()
        return carry

    def wait_col(i, carry):
        col_copy(i).wait_recv()
        return carry

    lax.fori_loop(1, n_grp, start_row, 0)
    copies = []
    for i, ((step_cols, step_grp), first, blocks, slot) in enumerate(placed):
        copy = pltpu.make_async_remote_copy(
            src_ref=blk.at[pl.ds(first, blocks)], dst_ref=blk.at[pl.ds(slot, blocks)],
            send_sem=send_sem.at[i], recv_sem=recv_sem.at[i],
            device_id=at(-step_cols, -step_grp), device_id_type=MESH,
        )
        copy.start()
        copies.append(copy)

    lax.fori_loop(1, n_grp, wait_row, 0)
    col_sums[0] = jnp.sum(row_sums[...], axis=0)
    lax.fori_loop(1, n_cols, start_col, 0)
    lax.fori_loop(1, n_cols, wait_col, 0)
    sum_squares = jnp.sum(jnp.sum(col_sums[...], axis=0), keepdims=True)
    rows_total = width * n_cols * n_grp
    inverse = 0.5 * lax.rsqrt(sum_squares / rows_total + 1e-06)

    count = cnt[0, 0]
    ids = [nbr[0, 0, p] for p in range(SLOTS)]

    def put(p, q, value):
        top = value.astype(jnp.bfloat16)
        rows, columns = pl.ds(p * width, width), pl.ds(q * width, width)
        high[rows, columns] = top
        low[rows, columns] = (value - top.astype(jnp.float32)).astype(jnp.bfloat16)

    for copy in copies:
        copy.wait_recv()

    for p in range(SLOTS):
        for q in range(p + 1):
            code = table[ids[p] * STENCIL + ids[q]]
            usable = (code < MISSING) & (p < count)
            turned = (code >= TURNED) & (code < MISSING)
            slot = lax.rem(code, TURNED)
            block = blk[slot]
            block = jnp.where(usable, block, 0.0)
            if p == q:
                put(p, q, block)
            else:
                other = block.T
                put(p, q, jnp.where(turned, other, block))
                put(q, p, jnp.where(turned, block, other))

    def times(vector):
        top = vector.astype(jnp.bfloat16)
        rest = (vector - top.astype(jnp.float32)).astype(jnp.bfloat16)
        both = jnp.concatenate([top, rest], axis=1)
        main = jnp.dot(high[...], both, preferred_element_type=jnp.float32)
        side = jnp.dot(low[...], top, preferred_element_type=jnp.float32)
        return (main[:, :width] + (main[:, width:] + side)) * inverse

    first = high[:, pl.ds(0, width)].astype(jnp.float32) + low[:, pl.ds(0, width)].astype(jnp.float32)
    initial = first * inverse
    column = 1.5 * initial - 0.5 * times(times(initial))
    image = column
    for _ in range(2):
        once = times(image)
        image = 1.5 * once - 0.5 * times(times(once))
    sign = 1.5 * column - 0.5 * image
    diagonal = lax.broadcasted_iota(jnp.int32, sign.shape, 0) == lax.broadcasted_iota(
        jnp.int32, sign.shape, 1
    )
    dens[...] = (0.5 * (jnp.where(diagonal, 1.0, 0.0) - sign)).reshape(dens.shape)

    for k in range(STENCIL):
        place, named = jnp.int32(0), jnp.int32(0)
        for p in range(SLOTS):
            hit = ((ids[p] == k) & (p < count)).astype(jnp.int32)
            place, named = place + p * hit, named + hit
        out[0, 0, k] = jnp.where(named > 0, dens[place], 0.0)

    def done_row(i, carry):
        row_copy(i).wait_send()
        return carry

    def done_col(i, carry):
        col_copy(i).wait_send()
        return carry

    for copy in copies:
        copy.wait_send()
    lax.fori_loop(1, n_grp, done_row, 0)
    lax.fori_loop(1, n_cols, done_col, 0)


def shards(hcols, neighbours, counts, n_cols, n_grp):
    width = hcols.shape[-1]
    placed, slots = transfers()
    order = SLOTS * width
    dma = pltpu.SemaphoreType.DMA
    return pl.pallas_call(
        functools.partial(kernel, n_cols, n_grp),
        out_shape=jax.ShapeDtypeStruct(hcols.shape, jnp.float32),
        in_specs=[
            pl.BlockSpec(memory_space=pl.ANY),
            pl.BlockSpec(memory_space=pltpu.SMEM),
            pl.BlockSpec(memory_space=pltpu.SMEM),
        ],
        out_specs=pl.BlockSpec(memory_space=pltpu.VMEM),
        scratch_shapes=[
            pltpu.VMEM((slots, width, width), jnp.float32),
            pltpu.SMEM((STENCIL * STENCIL,), jnp.int32),
            pltpu.VMEM((order, order), jnp.bfloat16),
            pltpu.VMEM((order, order), jnp.bfloat16),
            pltpu.VMEM((SLOTS, width, width), jnp.float32),
            pltpu.VMEM((n_grp, 8, width), jnp.float32),
            pltpu.VMEM((n_cols, 8, width), jnp.float32),
            dma,
            dma((len(placed),)),
            dma((len(placed),)),
            dma((n_grp,)),
            dma((n_grp,)),
            dma((n_cols,)),
            dma((n_cols,)),
        ],
        compiler_params=pltpu.CompilerParams(
            collective_id=0, has_side_effects=True, vmem_limit_bytes=32 * 1024 * 1024
        ),
        name="density_columns",
    )(hcols, neighbours, counts)


def solution(mesh):
    in_specs = (P("cols", "grp", None, None, None), P("cols", "grp", None), P("cols", "grp"))
    out_specs = P("cols", "grp", None, None, None)
    body = functools.partial(shards, n_cols=mesh.shape["cols"], n_grp=mesh.shape["grp"])
    return jax.shard_map(body, mesh=mesh, in_specs=in_specs, out_specs=out_specs, check_vma=False)
```

```python
import functools

import jax
import jax.numpy as jnp
from jax import lax
from jax.experimental import pallas as pl
from jax.experimental.pallas import tpu as pltpu
from jax.sharding import PartitionSpec as P

MESH = pl.DeviceIdType.MESH
SLOTS = 6
STENCIL = 9
MISSING = 64
TURNED = 32


def transfers():
    plan = []
    for along_cols in (-1, 1):
        plan.append(((along_cols, 0), 3, 3))
    for along_cols in (-1, 1):
        for along_grp in (-1, 1):
            plan.append(((along_cols, along_grp), 4, 1))
    for along_grp, runs in ((1, ((0, 2), (4, 1), (6, 2))), (-1, ((1, 2), (4, 1), (7, 2)))):
        for first, blocks in runs:
            plan.append(((0, along_grp), first, blocks))
    placed, slot = [], STENCIL
    for offset, first, blocks in plan:
        placed.append((offset, first, blocks, slot))
        slot += blocks
    return placed, slot


def lookup(placed):
    table = [MISSING] * (STENCIL * STENCIL)
    held = [((0, 0), k, k) for k in range(STENCIL)]
    for offset, first, blocks, slot in placed:
        held += [(offset, first + i, slot + i) for i in range(blocks)]
    for (cols, grp), k, slot in held:
        row_cols, row_grp = cols + k // 3 - 1, grp + k % 3 - 1
        assert abs(row_cols) <= 1 and abs(row_grp) <= 1
        column = (cols + 1) * 3 + grp + 1
        row = (row_cols + 1) * 3 + row_grp + 1
        table[row * STENCIL + column] = slot
        if row != column:
            table[column * STENCIL + row] = slot + TURNED
    return table


def kernel(
    n_cols, n_grp, hcols, nbr_hbm, cnt_hbm, out, nbr, cnt, blk, table, high, low, dens, row_sums, col_sums,
    small_sem, load_sem, send_sem, recv_sem, row_send, row_recv, col_send, col_recv,
):
    width = blk.shape[-1]
    placed, _ = transfers()
    col, grp = lax.axis_index("cols"), lax.axis_index("grp")

    def at(step_cols, step_grp):
        return (lax.rem(col + step_cols + n_cols, n_cols), lax.rem(grp + step_grp + n_grp, n_grp))

    odd = lax.rem(grp, 2)
    side = 1 - 2 * odd
    straight = {offset[0]: slot for offset, _, _, slot in placed if offset[1] == 0}
    corner = {offset: slot for offset, _, _, slot in placed if 0 not in offset}
    load = pltpu.make_async_copy(hcols.at[0, 0], blk.at[pl.ds(0, STENCIL)], load_sem)
    load.start()
    small = [
        pltpu.make_async_copy(nbr_hbm, nbr, small_sem.at[0]),
        pltpu.make_async_copy(cnt_hbm, cnt, small_sem.at[1]),
    ]
    for copy in small:
        copy.start()
    barrier = pltpu.get_barrier_semaphore()

    def greet_row(i, carry):
        pl.semaphore_signal(barrier, inc=1, device_id=at(0, i), device_id_type=MESH)
        return carry

    def greet_col(i, carry):
        pl.semaphore_signal(barrier, inc=1, device_id=at(i, 0), device_id_type=MESH)
        return carry

    lax.fori_loop(1, n_grp, greet_row, 0)
    lax.fori_loop(1, n_cols, greet_col, 0)
    for step_cols in (-1, 1):
        for step_grp in (-1, 1):
            pl.semaphore_signal(
                barrier, inc=1, device_id=at(step_cols, step_grp), device_id_type=MESH
            )
    for i, value in enumerate(lookup(placed)):
        table[i] = jnp.int32(value)
    even = 1 - odd
    for swapped, step_cols, step_grp in ((even, -1, 1), (odd, 1, -1)):
        near, far = (step_cols + 1) * 3 + 1, (step_cols + 1) * 3 + step_grp + 1
        place = straight[step_cols] + step_grp + 1
        table[far * STENCIL + near] = place + TURNED * swapped
        table[near * STENCIL + far] = place + TURNED * (1 - swapped)
    for copy in small:
        copy.wait()
    load.wait()
    own = jnp.zeros((8, width), jnp.float32)
    for k in range(STENCIL):
        part = blk[k]
        own = own + jnp.sum((part * part).reshape(width // 8, 8, width), axis=0)
    row_sums[0] = own
    pl.semaphore_wait(barrier, n_grp + n_cols + 2)

    def row_copy(i):
        return pltpu.make_async_remote_copy(
            src_ref=row_sums.at[0], dst_ref=row_sums.at[i], send_sem=row_send.at[i],
            recv_sem=row_recv.at[i], device_id=at(0, i), device_id_type=MESH,
        )

    def col_copy(i):
        return pltpu.make_async_remote_copy(
            src_ref=col_sums.at[0], dst_ref=col_sums.at[i], send_sem=col_send.at[i],
            recv_sem=col_recv.at[i], device_id=at(i, 0), device_id_type=MESH,
        )

    def start_row(i, carry):
        row_copy(i).start()
        return carry

    def start_col(i, carry):
        col_copy(i).start()
        return carry

    def wait_row(i, carry):
        row_copy(i).wait_recv()
        return carry

    def wait_col(i, carry):
        col_copy(i).wait_recv()
        return carry

    lax.fori_loop(1, n_grp, start_row, 0)
    copies = []

    def push(source, target, blocks, step_cols, step_grp):
        i = len(copies)
        copy = pltpu.make_async_remote_copy(
            src_ref=blk.at[pl.ds(source, blocks)], dst_ref=blk.at[pl.ds(target, blocks)],
            send_sem=send_sem.at[i], recv_sem=recv_sem.at[i],
            device_id=at(step_cols, step_grp), device_id_type=MESH,
        )
        copy.start()
        copies.append(copy)
        return copy

    def pick(at_even, at_odd):
        return at_even + (at_odd - at_even) * odd

    whole_edge = push(3, pick(straight[1], straight[-1]), 3, -side, 0)
    half_edge = push(3 + odd, pick(straight[-1], straight[1]) + odd, 2, side, 0)
    for step_cols in (-1, 1):
        push(4, pick(corner[-step_cols, 1], corner[-step_cols, -1]), 1, step_cols, -side)
    for offset, first, blocks, slot in placed:
        if offset[0] == 0:
            push(first, slot, blocks, 0, -offset[1])

    lax.fori_loop(1, n_grp, wait_row, 0)
    col_sums[0] = jnp.sum(row_sums[...], axis=0)
    lax.fori_loop(1, n_cols, start_col, 0)

    count = cnt[0, 0]
    ids = [nbr[0, 0, p] for p in range(SLOTS)]

    def put(p, q, value):
        top = value.astype(jnp.bfloat16)
        rows, columns = pl.ds(p * width, width), pl.ds(q * width, width)
        high[rows, columns] = top
        low[rows, columns] = (value - top.astype(jnp.float32)).astype(jnp.bfloat16)

    whole_edge.wait_recv()
    push(
        pick(straight[1] + 1, straight[-1] + 1), pick(corner[1, -1], corner[-1, 1]), 1, 0, side
    )
    push(
        pick(straight[1] + 2, straight[-1]), pick(straight[1], straight[-1] + 2), 1, 0, side
    )
    half_edge.wait_recv()
    push(
        pick(straight[-1] + 1, straight[1] + 1), pick(corner[-1, -1], corner[1, 1]), 1, 0, side
    )
    for copy in copies:
        if copy is not whole_edge and copy is not half_edge:
            copy.wait_recv()

    for p in range(SLOTS):
        for q in range(p + 1):
            code = table[ids[p] * STENCIL + ids[q]]
            usable = (code < MISSING) & (p < count)
            turned = (code >= TURNED) & (code < MISSING)
            slot = lax.rem(code, TURNED)
            block = blk[slot]
            block = jnp.where(usable, block, 0.0)
            if p == q:
                put(p, q, block)
            else:
                other = block.T
                put(p, q, jnp.where(turned, other, block))
                put(q, p, jnp.where(turned, block, other))

    lax.fori_loop(1, n_cols, wait_col, 0)
    sum_squares = jnp.sum(jnp.sum(col_sums[...], axis=0), keepdims=True)
    rows_total = width * n_cols * n_grp
    inverse = 0.5 * lax.rsqrt(sum_squares / rows_total + 1e-06)

    def times(vector):
        top = vector.astype(jnp.bfloat16)
        rest = (vector - top.astype(jnp.float32)).astype(jnp.bfloat16)
        both = jnp.concatenate([top, rest], axis=1)
        main = jnp.dot(high[...], both, preferred_element_type=jnp.float32)
        side = jnp.dot(low[...], top, preferred_element_type=jnp.float32)
        return (main[:, :width] + (main[:, width:] + side)) * inverse

    first = high[:, pl.ds(0, width)].astype(jnp.float32) + low[:, pl.ds(0, width)].astype(jnp.float32)
    initial = first * inverse
    column = 1.5 * initial - 0.5 * times(times(initial))
    image = column
    for _ in range(2):
        once = times(image)
        image = 1.5 * once - 0.5 * times(times(once))
    sign = 1.5 * column - 0.5 * image
    diagonal = lax.broadcasted_iota(jnp.int32, sign.shape, 0) == lax.broadcasted_iota(
        jnp.int32, sign.shape, 1
    )
    dens[...] = (0.5 * (jnp.where(diagonal, 1.0, 0.0) - sign)).reshape(dens.shape)

    for k in range(STENCIL):
        place, named = jnp.int32(0), jnp.int32(0)
        for p in range(SLOTS):
            hit = ((ids[p] == k) & (p < count)).astype(jnp.int32)
            place, named = place + p * hit, named + hit
        out[0, 0, k] = jnp.where(named > 0, dens[place], 0.0)

    def done_row(i, carry):
        row_copy(i).wait_send()
        return carry

    def done_col(i, carry):
        col_copy(i).wait_send()
        return carry

    for copy in copies:
        copy.wait_send()
    lax.fori_loop(1, n_grp, done_row, 0)
    lax.fori_loop(1, n_cols, done_col, 0)


def shards(hcols, neighbours, counts, n_cols, n_grp):
    width = hcols.shape[-1]
    placed, slots = transfers()
    order = SLOTS * width
    dma = pltpu.SemaphoreType.DMA
    return pl.pallas_call(
        functools.partial(kernel, n_cols, n_grp),
        out_shape=jax.ShapeDtypeStruct(hcols.shape, jnp.float32),
        in_specs=[
            pl.BlockSpec(memory_space=pltpu.HBM),
            pl.BlockSpec(memory_space=pltpu.HBM),
            pl.BlockSpec(memory_space=pltpu.HBM),
        ],
        out_specs=pl.BlockSpec(memory_space=pltpu.VMEM),
        scratch_shapes=[
            pltpu.SMEM(neighbours.shape, jnp.int32),
            pltpu.SMEM(counts.shape, jnp.int32),
            pltpu.VMEM((slots, width, width), jnp.float32),
            pltpu.SMEM((STENCIL * STENCIL,), jnp.int32),
            pltpu.VMEM((order, order), jnp.bfloat16),
            pltpu.VMEM((order, order), jnp.bfloat16),
            pltpu.VMEM((SLOTS, width, width), jnp.float32),
            pltpu.VMEM((n_grp, 8, width), jnp.float32),
            pltpu.VMEM((n_cols, 8, width), jnp.float32),
            dma((2,)),
            dma,
            dma((len(placed) + 1,)),
            dma((len(placed) + 1,)),
            dma((n_grp,)),
            dma((n_grp,)),
            dma((n_cols,)),
            dma((n_cols,)),
        ],
        compiler_params=pltpu.CompilerParams(
            collective_id=0, has_side_effects=True, vmem_limit_bytes=63 * 1024 * 1024
        ),
        name="density_columns",
    )(hcols, neighbours, counts)


def solution(mesh):
    in_specs = (P("cols", "grp", None, None, None), P("cols", "grp", None), P("cols", "grp"))
    out_specs = P("cols", "grp", None, None, None)
    body = functools.partial(shards, n_cols=mesh.shape["cols"], n_grp=mesh.shape["grp"])
    return jax.shard_map(body, mesh=mesh, in_specs=in_specs, out_specs=out_specs, check_vma=False)
```

```python
import functools

import jax
import jax.numpy as jnp
from jax import lax
from jax.experimental import pallas as pl
from jax.experimental.pallas import tpu as pltpu
from jax.sharding import PartitionSpec as P

MESH = pl.DeviceIdType.MESH
SLOTS = 6
STENCIL = 9
MISSING = 64
TURNED = 32


def transfers():
    plan = []
    for along_cols in (-1, 1):
        plan.append(((along_cols, 0), 3, 3))
    for along_cols in (-1, 1):
        for along_grp in (-1, 1):
            plan.append(((along_cols, along_grp), 4, 1))
    for along_grp, runs in ((1, ((0, 2), (4, 1), (6, 2))), (-1, ((1, 2), (4, 1), (7, 2)))):
        for first, blocks in runs:
            plan.append(((0, along_grp), first, blocks))
    placed, slot = [], STENCIL
    for offset, first, blocks in plan:
        placed.append((offset, first, blocks, slot))
        slot += blocks
    return placed, slot


def lookup(placed):
    table = [MISSING] * (STENCIL * STENCIL)
    held = [((0, 0), k, k) for k in range(STENCIL)]
    for offset, first, blocks, slot in placed:
        held += [(offset, first + i, slot + i) for i in range(blocks)]
    for (cols, grp), k, slot in held:
        row_cols, row_grp = cols + k // 3 - 1, grp + k % 3 - 1
        assert abs(row_cols) <= 1 and abs(row_grp) <= 1
        column = (cols + 1) * 3 + grp + 1
        row = (row_cols + 1) * 3 + row_grp + 1
        table[row * STENCIL + column] = slot
        if row != column:
            table[column * STENCIL + row] = slot + TURNED
    return table


def kernel(
    n_cols, n_grp, hcols, nbr_hbm, cnt_hbm, out, nbr, cnt, blk, table, high, low, dens, row_sums, col_sums,
    small_sem, load_sem, send_sem, recv_sem, row_send, row_recv, col_send, col_recv,
):
    width = blk.shape[-1]
    placed, _ = transfers()
    col, grp = lax.axis_index("cols"), lax.axis_index("grp")

    def at(step_cols, step_grp):
        return (lax.rem(col + step_cols + n_cols, n_cols), lax.rem(grp + step_grp + n_grp, n_grp))

    odd = lax.rem(grp, 2)
    side = 1 - 2 * odd
    straight = {offset[0]: slot for offset, _, _, slot in placed if offset[1] == 0}
    corner = {offset: slot for offset, _, _, slot in placed if 0 not in offset}
    load = pltpu.make_async_copy(hcols.at[0, 0], blk.at[pl.ds(0, STENCIL)], load_sem)
    load.start()
    small = [
        pltpu.make_async_copy(nbr_hbm, nbr, small_sem.at[0]),
        pltpu.make_async_copy(cnt_hbm, cnt, small_sem.at[1]),
    ]
    for copy in small:
        copy.start()
    barrier = pltpu.get_barrier_semaphore()

    def greet_row(i, carry):
        pl.semaphore_signal(barrier, inc=1, device_id=at(0, i), device_id_type=MESH)
        return carry

    def greet_col(i, carry):
        pl.semaphore_signal(barrier, inc=1, device_id=at(i, 0), device_id_type=MESH)
        return carry

    lax.fori_loop(1, n_grp, greet_row, 0)
    lax.fori_loop(1, n_cols, greet_col, 0)
    for step_cols in (-1, 1):
        for step_grp in (-1, 1):
            pl.semaphore_signal(
                barrier, inc=1, device_id=at(step_cols, step_grp), device_id_type=MESH
            )
    for i, value in enumerate(lookup(placed)):
        table[i] = jnp.int32(value)
    even = 1 - odd
    for swapped, step_cols, step_grp in ((even, -1, 1), (odd, 1, -1)):
        near, far = (step_cols + 1) * 3 + 1, (step_cols + 1) * 3 + step_grp + 1
        place = straight[step_cols] + step_grp + 1
        table[far * STENCIL + near] = place + TURNED * swapped
        table[near * STENCIL + far] = place + TURNED * (1 - swapped)
    for copy in small:
        copy.wait()
    load.wait()
    own = jnp.zeros((8, width), jnp.float32)
    for k in range(STENCIL):
        part = blk[k]
        own = own + jnp.sum((part * part).reshape(width // 8, 8, width), axis=0)
    row_sums[0] = own
    pl.semaphore_wait(barrier, n_grp + n_cols + 2)

    def row_copy(i):
        return pltpu.make_async_remote_copy(
            src_ref=row_sums.at[0], dst_ref=row_sums.at[i], send_sem=row_send.at[i],
            recv_sem=row_recv.at[i], device_id=at(0, i), device_id_type=MESH,
        )

    def col_copy(i):
        return pltpu.make_async_remote_copy(
            src_ref=col_sums.at[0], dst_ref=col_sums.at[i], send_sem=col_send.at[i],
            recv_sem=col_recv.at[i], device_id=at(i, 0), device_id_type=MESH,
        )

    def start_row(i, carry):
        row_copy(i).start()
        return carry

    def start_col(i, carry):
        col_copy(i).start()
        return carry

    def wait_row(i, carry):
        row_copy(i).wait_recv()
        return carry

    def wait_col(i, carry):
        col_copy(i).wait_recv()
        return carry

    lax.fori_loop(1, n_grp, start_row, 0)
    copies = []

    def push(source, target, blocks, step_cols, step_grp):
        i = len(copies)
        copy = pltpu.make_async_remote_copy(
            src_ref=blk.at[pl.ds(source, blocks)], dst_ref=blk.at[pl.ds(target, blocks)],
            send_sem=send_sem.at[i], recv_sem=recv_sem.at[i],
            device_id=at(step_cols, step_grp), device_id_type=MESH,
        )
        copy.start()
        copies.append(copy)
        return copy

    def pick(at_even, at_odd):
        return at_even + (at_odd - at_even) * odd

    whole_edge = push(3, pick(straight[1], straight[-1]), 3, -side, 0)
    half_edge = push(3 + odd, pick(straight[-1], straight[1]) + odd, 2, side, 0)
    for step_cols in (-1, 1):
        push(4, pick(corner[-step_cols, 1], corner[-step_cols, -1]), 1, step_cols, -side)
    for offset, first, blocks, slot in placed:
        if offset[0] == 0:
            push(first, slot, blocks, 0, -offset[1])

    lax.fori_loop(1, n_grp, wait_row, 0)
    col_sums[0] = jnp.sum(row_sums[...], axis=0)
    lax.fori_loop(1, n_cols, start_col, 0)

    count = cnt[0, 0]
    ids = [nbr[0, 0, p] for p in range(SLOTS)]

    def put(p, q, value):
        top = value.astype(jnp.bfloat16)
        rows, columns = pl.ds(p * width, width), pl.ds(q * width, width)
        high[rows, columns] = top
        low[rows, columns] = (value - top.astype(jnp.float32)).astype(jnp.bfloat16)

    whole_edge.wait_recv()
    push(
        pick(straight[1] + 1, straight[-1] + 1), pick(corner[1, -1], corner[-1, 1]), 1, 0, side
    )
    push(
        pick(straight[1] + 2, straight[-1]), pick(straight[1], straight[-1] + 2), 1, 0, side
    )
    half_edge.wait_recv()
    push(
        pick(straight[-1] + 1, straight[1] + 1), pick(corner[-1, -1], corner[1, 1]), 1, 0, side
    )
    for copy in copies:
        if copy is not whole_edge and copy is not half_edge:
            copy.wait_recv()

    for p in range(SLOTS):
        for q in range(p + 1):
            code = table[ids[p] * STENCIL + ids[q]]
            usable = (code < MISSING) & (p < count)
            turned = (code >= TURNED) & (code < MISSING)
            slot = lax.rem(code, TURNED)
            block = blk[slot]
            block = jnp.where(usable, block, 0.0)
            if p == q:
                put(p, q, block)
            else:
                other = block.T
                put(p, q, jnp.where(turned, other, block))
                put(q, p, jnp.where(turned, block, other))

    lax.fori_loop(1, n_cols, wait_col, 0)
    sum_squares = jnp.sum(jnp.sum(col_sums[...], axis=0), keepdims=True)
    rows_total = width * n_cols * n_grp
    inverse = 0.5 * lax.rsqrt(sum_squares / rows_total + 1e-06)

    def times(vector):
        top = vector.astype(jnp.bfloat16)
        rest = (vector - top.astype(jnp.float32)).astype(jnp.bfloat16)
        both = jnp.concatenate([top, rest], axis=1)
        main = jnp.dot(high[...], both, preferred_element_type=jnp.float32)
        side = jnp.dot(low[...], top, preferred_element_type=jnp.float32)
        return (main[:, :width] + (main[:, width:] + side)) * inverse

    first = high[:, pl.ds(0, width)].astype(jnp.float32) + low[:, pl.ds(0, width)].astype(jnp.float32)
    initial = first * inverse
    column = 1.5 * initial - 0.5 * times(times(initial))
    image = column
    for _ in range(2):
        once = times(image)
        image = 1.5 * once - 0.5 * times(times(once))
    sign = 1.5 * column - 0.5 * image
    diagonal = lax.broadcasted_iota(jnp.int32, sign.shape, 0) == lax.broadcasted_iota(
        jnp.int32, sign.shape, 1
    )
    dens[...] = (0.5 * (jnp.where(diagonal, 1.0, 0.0) - sign)).reshape(dens.shape)

    for k in range(STENCIL):
        place, named = jnp.int32(0), jnp.int32(0)
        for p in range(SLOTS):
            hit = ((ids[p] == k) & (p < count)).astype(jnp.int32)
            place, named = place + p * hit, named + hit
        out[0, 0, k] = jnp.where(named > 0, dens[place], 0.0)

    def done_row(i, carry):
        row_copy(i).wait_send()
        return carry

    def done_col(i, carry):
        col_copy(i).wait_send()
        return carry

    for copy in copies:
        copy.wait_send()
    lax.fori_loop(1, n_grp, done_row, 0)
    lax.fori_loop(1, n_cols, done_col, 0)


def shards(hcols, neighbours, counts, n_cols, n_grp):
    width = hcols.shape[-1]
    placed, slots = transfers()
    order = SLOTS * width
    dma = pltpu.SemaphoreType.DMA
    hcols, neighbours = (
        pltpu.with_memory_space_constraint(each, pltpu.HBM) for each in (hcols, neighbours)
    )
    return pl.pallas_call(
        functools.partial(kernel, n_cols, n_grp),
        out_shape=jax.ShapeDtypeStruct(hcols.shape, jnp.float32),
        in_specs=[
            pl.BlockSpec(memory_space=pltpu.HBM),
            pl.BlockSpec(memory_space=pltpu.HBM),
            pl.BlockSpec(memory_space=pltpu.HBM),
        ],
        out_specs=pl.BlockSpec(memory_space=pltpu.VMEM),
        scratch_shapes=[
            pltpu.SMEM(neighbours.shape, jnp.int32),
            pltpu.SMEM(counts.shape, jnp.int32),
            pltpu.VMEM((slots, width, width), jnp.float32),
            pltpu.SMEM((STENCIL * STENCIL,), jnp.int32),
            pltpu.VMEM((order, order), jnp.bfloat16),
            pltpu.VMEM((order, order), jnp.bfloat16),
            pltpu.VMEM((SLOTS, width, width), jnp.float32),
            pltpu.VMEM((n_grp, 8, width), jnp.float32),
            pltpu.VMEM((n_cols, 8, width), jnp.float32),
            dma((2,)),
            dma,
            dma((len(placed) + 1,)),
            dma((len(placed) + 1,)),
            dma((n_grp,)),
            dma((n_grp,)),
            dma((n_cols,)),
            dma((n_cols,)),
        ],
        compiler_params=pltpu.CompilerParams(
            collective_id=0, has_side_effects=True, vmem_limit_bytes=24 * 1024 * 1024
        ),
        name="density_columns",
    )(hcols, neighbours, counts)


def solution(mesh):
    in_specs = (P("cols", "grp", None, None, None), P("cols", "grp", None), P("cols", "grp"))
    out_specs = P("cols", "grp", None, None, None)
    body = functools.partial(shards, n_cols=mesh.shape["cols"], n_grp=mesh.shape["grp"])
    return jax.shard_map(body, mesh=mesh, in_specs=in_specs, out_specs=out_specs, check_vma=False)
```

```python
import functools

import jax
import jax.numpy as jnp
from jax import lax
from jax.experimental import pallas as pl
from jax.experimental.pallas import tpu as pltpu
from jax.sharding import PartitionSpec as P

MESH = pl.DeviceIdType.MESH
SLOTS = 6
STENCIL = 9
MISSING = 64
TURNED = 32


def transfers():
    plan = []
    for along_cols in (-1, 1):
        plan.append(((along_cols, 0), 3, 3))
    for along_cols in (-1, 1):
        for along_grp in (-1, 1):
            plan.append(((along_cols, along_grp), 4, 1))
    for along_grp, runs in ((1, ((0, 2), (4, 1), (6, 2))), (-1, ((1, 2), (4, 1), (7, 2)))):
        for first, blocks in runs:
            plan.append(((0, along_grp), first, blocks))
    placed, slot = [], STENCIL
    for offset, first, blocks in plan:
        placed.append((offset, first, blocks, slot))
        slot += blocks
    return placed, slot


def lookup(placed):
    table = [MISSING] * (STENCIL * STENCIL)
    held = [((0, 0), k, k) for k in range(STENCIL)]
    for offset, first, blocks, slot in placed:
        held += [(offset, first + i, slot + i) for i in range(blocks)]
    for (cols, grp), k, slot in held:
        row_cols, row_grp = cols + k // 3 - 1, grp + k % 3 - 1
        assert abs(row_cols) <= 1 and abs(row_grp) <= 1
        column = (cols + 1) * 3 + grp + 1
        row = (row_cols + 1) * 3 + row_grp + 1
        table[row * STENCIL + column] = slot
        if row != column:
            table[column * STENCIL + row] = slot + TURNED
    return table


def kernel(
    n_cols, n_grp, hcols, nbr_hbm, cnt_hbm, out, nbr, cnt, blk, table, high, low, dens, row_sums, col_sums,
    small_sem, load_sem, send_sem, recv_sem, row_send, row_recv, col_send, col_recv,
):
    width = blk.shape[-1]
    placed, _ = transfers()
    col, grp = lax.axis_index("cols"), lax.axis_index("grp")

    def at(step_cols, step_grp):
        return (lax.rem(col + step_cols + n_cols, n_cols), lax.rem(grp + step_grp + n_grp, n_grp))

    odd = lax.rem(grp, 2)
    side = 1 - 2 * odd
    straight = {offset[0]: slot for offset, _, _, slot in placed if offset[1] == 0}
    corner = {offset: slot for offset, _, _, slot in placed if 0 not in offset}
    load = pltpu.make_async_copy(hcols.at[0, 0], blk.at[pl.ds(0, STENCIL)], load_sem)
    load.start()
    small = [
        pltpu.make_async_copy(nbr_hbm, nbr, small_sem.at[0]),
        pltpu.make_async_copy(cnt_hbm, cnt, small_sem.at[1]),
    ]
    for copy in small:
        copy.start()
    barrier = pltpu.get_barrier_semaphore()

    def greet_row(i, carry):
        pl.semaphore_signal(barrier, inc=1, device_id=at(0, i), device_id_type=MESH)
        return carry

    def greet_col(i, carry):
        pl.semaphore_signal(barrier, inc=1, device_id=at(i, 0), device_id_type=MESH)
        return carry

    lax.fori_loop(1, n_grp, greet_row, 0)
    lax.fori_loop(1, n_cols, greet_col, 0)
    for i, value in enumerate(lookup(placed)):
        table[i] = jnp.int32(value)
    even = 1 - odd
    for swapped, step_cols, step_grp in ((even, -1, 1), (odd, 1, -1)):
        near, far = (step_cols + 1) * 3 + 1, (step_cols + 1) * 3 + step_grp + 1
        place = straight[step_cols] + step_grp + 1
        table[far * STENCIL + near] = place + TURNED * swapped
        table[near * STENCIL + far] = place + TURNED * (1 - swapped)
    for copy in small:
        copy.wait()
    load.wait()
    own = jnp.zeros((8, width), jnp.float32)
    for k in range(STENCIL):
        part = blk[k]
        own = own + jnp.sum((part * part).reshape(width // 8, 8, width), axis=0)
    row_sums[0] = own
    pl.semaphore_wait(barrier, n_grp + n_cols - 2)

    def row_copy(i):
        return pltpu.make_async_remote_copy(
            src_ref=row_sums.at[0], dst_ref=row_sums.at[i], send_sem=row_send.at[i],
            recv_sem=row_recv.at[i], device_id=at(0, i), device_id_type=MESH,
        )

    def col_copy(i):
        return pltpu.make_async_remote_copy(
            src_ref=col_sums.at[0], dst_ref=col_sums.at[i], send_sem=col_send.at[i],
            recv_sem=col_recv.at[i], device_id=at(i, 0), device_id_type=MESH,
        )

    def start_row(i, carry):
        row_copy(i).start()
        return carry

    def start_col(i, carry):
        col_copy(i).start()
        return carry

    def wait_row(i, carry):
        row_copy(i).wait_recv()
        return carry

    def wait_col(i, carry):
        col_copy(i).wait_recv()
        return carry

    lax.fori_loop(1, n_grp, start_row, 0)
    copies = []

    def push(source, target, blocks, step_cols, step_grp):
        i = len(copies)
        copy = pltpu.make_async_remote_copy(
            src_ref=blk.at[pl.ds(source, blocks)], dst_ref=blk.at[pl.ds(target, blocks)],
            send_sem=send_sem.at[i], recv_sem=recv_sem.at[i],
            device_id=at(step_cols, step_grp), device_id_type=MESH,
        )
        copy.start()
        copies.append(copy)
        return copy

    def pick(at_even, at_odd):
        return at_even + (at_odd - at_even) * odd

    whole_edge = push(3, pick(straight[1], straight[-1]), 3, -side, 0)
    half_edge = push(3 + odd, pick(straight[-1], straight[1]) + odd, 2, side, 0)
    for offset, first, blocks, slot in placed:
        if offset[0] == 0:
            push(first, slot, blocks, 0, -offset[1])

    lax.fori_loop(1, n_grp, wait_row, 0)
    col_sums[0] = jnp.sum(row_sums[...], axis=0)
    lax.fori_loop(1, n_cols, start_col, 0)

    count = cnt[0, 0]
    ids = [nbr[0, 0, p] for p in range(SLOTS)]

    def put(p, q, value):
        top = value.astype(jnp.bfloat16)
        rows, columns = pl.ds(p * width, width), pl.ds(q * width, width)
        high[rows, columns] = top
        low[rows, columns] = (value - top.astype(jnp.float32)).astype(jnp.bfloat16)

    whole_edge.wait_recv()
    push(
        pick(straight[1] + 1, straight[-1] + 1), pick(corner[1, -1], corner[-1, 1]), 1, 0, side
    )
    push(
        pick(straight[1] + 2, straight[-1]), pick(straight[1], straight[-1] + 2), 1, 0, side
    )
    push(pick(straight[1] + 1, straight[-1] + 1), pick(corner[1, 1], corner[-1, -1]), 1, 0, -side)
    half_edge.wait_recv()
    push(
        pick(straight[-1] + 1, straight[1] + 1), pick(corner[-1, 1], corner[1, -1]), 1, 0, -side
    )
    push(
        pick(straight[-1] + 1, straight[1] + 1), pick(corner[-1, -1], corner[1, 1]), 1, 0, side
    )
    for copy in copies:
        if copy is not whole_edge and copy is not half_edge:
            copy.wait_recv()

    for p in range(SLOTS):
        for q in range(p + 1):
            code = table[ids[p] * STENCIL + ids[q]]
            usable = (code < MISSING) & (p < count)
            turned = (code >= TURNED) & (code < MISSING)
            slot = lax.rem(code, TURNED)
            block = blk[slot]
            block = jnp.where(usable, block, 0.0)
            if p == q:
                put(p, q, block)
            else:
                other = block.T
                put(p, q, jnp.where(turned, other, block))
                put(q, p, jnp.where(turned, block, other))

    lax.fori_loop(1, n_cols, wait_col, 0)
    sum_squares = jnp.sum(jnp.sum(col_sums[...], axis=0), keepdims=True)
    rows_total = width * n_cols * n_grp
    inverse = 0.5 * lax.rsqrt(sum_squares / rows_total + 1e-06)

    def times(vector):
        top = vector.astype(jnp.bfloat16)
        rest = (vector - top.astype(jnp.float32)).astype(jnp.bfloat16)
        both = jnp.concatenate([top, rest], axis=1)
        main = jnp.dot(high[...], both, preferred_element_type=jnp.float32)
        side = jnp.dot(low[...], top, preferred_element_type=jnp.float32)
        return (main[:, :width] + (main[:, width:] + side)) * inverse

    first = high[:, pl.ds(0, width)].astype(jnp.float32) + low[:, pl.ds(0, width)].astype(jnp.float32)
    initial = first * inverse
    column = 1.5 * initial - 0.5 * times(times(initial))
    image = column
    for _ in range(2):
        once = times(image)
        image = 1.5 * once - 0.5 * times(times(once))
    sign = 1.5 * column - 0.5 * image
    diagonal = lax.broadcasted_iota(jnp.int32, sign.shape, 0) == lax.broadcasted_iota(
        jnp.int32, sign.shape, 1
    )
    dens[...] = (0.5 * (jnp.where(diagonal, 1.0, 0.0) - sign)).reshape(dens.shape)

    for k in range(STENCIL):
        place, named = jnp.int32(0), jnp.int32(0)
        for p in range(SLOTS):
            hit = ((ids[p] == k) & (p < count)).astype(jnp.int32)
            place, named = place + p * hit, named + hit
        out[0, 0, k] = jnp.where(named > 0, dens[place], 0.0)

    def done_row(i, carry):
        row_copy(i).wait_send()
        return carry

    def done_col(i, carry):
        col_copy(i).wait_send()
        return carry

    for copy in copies:
        copy.wait_send()
    lax.fori_loop(1, n_grp, done_row, 0)
    lax.fori_loop(1, n_cols, done_col, 0)


def shards(hcols, neighbours, counts, n_cols, n_grp):
    width = hcols.shape[-1]
    placed, slots = transfers()
    order = SLOTS * width
    dma = pltpu.SemaphoreType.DMA
    hcols, neighbours = (
        pltpu.with_memory_space_constraint(each, pltpu.HBM) for each in (hcols, neighbours)
    )
    return pl.pallas_call(
        functools.partial(kernel, n_cols, n_grp),
        out_shape=jax.ShapeDtypeStruct(hcols.shape, jnp.float32),
        in_specs=[
            pl.BlockSpec(memory_space=pltpu.HBM),
            pl.BlockSpec(memory_space=pltpu.HBM),
            pl.BlockSpec(memory_space=pltpu.HBM),
        ],
        out_specs=pl.BlockSpec(memory_space=pltpu.VMEM),
        scratch_shapes=[
            pltpu.SMEM(neighbours.shape, jnp.int32),
            pltpu.SMEM(counts.shape, jnp.int32),
            pltpu.VMEM((slots, width, width), jnp.float32),
            pltpu.SMEM((STENCIL * STENCIL,), jnp.int32),
            pltpu.VMEM((order, order), jnp.bfloat16),
            pltpu.VMEM((order, order), jnp.bfloat16),
            pltpu.VMEM((SLOTS, width, width), jnp.float32),
            pltpu.VMEM((n_grp, 8, width), jnp.float32),
            pltpu.VMEM((n_cols, 8, width), jnp.float32),
            dma((2,)),
            dma,
            dma((len(placed) + 1,)),
            dma((len(placed) + 1,)),
            dma((n_grp,)),
            dma((n_grp,)),
            dma((n_cols,)),
            dma((n_cols,)),
        ],
        compiler_params=pltpu.CompilerParams(
            collective_id=0, has_side_effects=True, vmem_limit_bytes=24 * 1024 * 1024
        ),
        name="density_columns",
    )(hcols, neighbours, counts)


def solution(mesh):
    in_specs = (P("cols", "grp", None, None, None), P("cols", "grp", None), P("cols", "grp"))
    out_specs = P("cols", "grp", None, None, None)
    body = functools.partial(shards, n_cols=mesh.shape["cols"], n_grp=mesh.shape["grp"])
    return jax.shard_map(body, mesh=mesh, in_specs=in_specs, out_specs=out_specs, check_vma=False)
```

```python
import functools

import jax
import jax.numpy as jnp
from jax import lax
from jax.experimental import pallas as pl
from jax.experimental.pallas import tpu as pltpu
from jax.sharding import PartitionSpec as P

MESH = pl.DeviceIdType.MESH
SLOTS = 6
STENCIL = 9
MISSING = 64
TURNED = 32


def transfers():
    plan = []
    for along_cols in (-1, 1):
        plan.append(((along_cols, 0), 3, 3))
    for along_cols in (-1, 1):
        for along_grp in (-1, 1):
            plan.append(((along_cols, along_grp), 4, 1))
    for along_grp, runs in ((1, ((0, 2), (4, 1), (6, 2))), (-1, ((1, 2), (4, 1), (7, 2)))):
        for first, blocks in runs:
            plan.append(((0, along_grp), first, blocks))
    placed, slot = [], STENCIL
    for offset, first, blocks in plan:
        placed.append((offset, first, blocks, slot))
        slot += blocks
    return placed, slot


def lookup(placed):
    table = [MISSING] * (STENCIL * STENCIL)
    held = [((0, 0), k, k) for k in range(STENCIL)]
    for offset, first, blocks, slot in placed:
        held += [(offset, first + i, slot + i) for i in range(blocks)]
    for (cols, grp), k, slot in held:
        row_cols, row_grp = cols + k // 3 - 1, grp + k % 3 - 1
        assert abs(row_cols) <= 1 and abs(row_grp) <= 1
        column = (cols + 1) * 3 + grp + 1
        row = (row_cols + 1) * 3 + row_grp + 1
        table[row * STENCIL + column] = slot
        if row != column:
            table[column * STENCIL + row] = slot + TURNED
    return table


def kernel(
    n_cols, n_grp, hcols, nbr_hbm, cnt_hbm, out, nbr, cnt, blk, table, high, low, dens, row_sums, col_sums,
    small_sem, load_sem, send_sem, recv_sem, row_send, row_recv, col_send, col_recv,
):
    width = blk.shape[-1]
    placed, _ = transfers()
    col, grp = lax.axis_index("cols"), lax.axis_index("grp")

    def at(step_cols, step_grp):
        return (lax.rem(col + step_cols + n_cols, n_cols), lax.rem(grp + step_grp + n_grp, n_grp))

    odd = lax.rem(grp, 2)
    side = 1 - 2 * odd
    straight = {offset[0]: slot for offset, _, _, slot in placed if offset[1] == 0}
    corner = {offset: slot for offset, _, _, slot in placed if 0 not in offset}
    load = pltpu.make_async_copy(hcols.at[0, 0], blk.at[pl.ds(0, STENCIL)], load_sem)
    load.start()
    small = [
        pltpu.make_async_copy(nbr_hbm, nbr, small_sem.at[0]),
        pltpu.make_async_copy(cnt_hbm, cnt, small_sem.at[1]),
    ]
    for copy in small:
        copy.start()
    barrier = pltpu.get_barrier_semaphore()

    def greet_row(i, carry):
        pl.semaphore_signal(barrier, inc=1, device_id=at(0, i), device_id_type=MESH)
        return carry

    def greet_col(i, carry):
        pl.semaphore_signal(barrier, inc=1, device_id=at(i, 0), device_id_type=MESH)
        return carry

    lax.fori_loop(1, n_grp, greet_row, 0)
    lax.fori_loop(1, n_cols, greet_col, 0)
    for i, value in enumerate(lookup(placed)):
        table[i] = jnp.int32(value)
    even = 1 - odd
    for swapped, step_cols, step_grp in ((even, -1, 1), (odd, 1, -1)):
        near, far = (step_cols + 1) * 3 + 1, (step_cols + 1) * 3 + step_grp + 1
        place = straight[step_cols] + step_grp + 1
        table[far * STENCIL + near] = place + TURNED * swapped
        table[near * STENCIL + far] = place + TURNED * (1 - swapped)
    for copy in small:
        copy.wait()
    load.wait()
    own = jnp.zeros((8, width), jnp.float32)
    for k in range(STENCIL):
        part = blk[k]
        own = own + jnp.sum((part * part).reshape(width // 8, 8, width), axis=0)
    row_sums[0] = own
    pl.semaphore_wait(barrier, n_grp + n_cols - 2)

    def row_copy(i):
        return pltpu.make_async_remote_copy(
            src_ref=row_sums.at[0], dst_ref=row_sums.at[i], send_sem=row_send.at[i],
            recv_sem=row_recv.at[i], device_id=at(0, i), device_id_type=MESH,
        )

    def col_copy(i):
        return pltpu.make_async_remote_copy(
            src_ref=col_sums.at[0], dst_ref=col_sums.at[i], send_sem=col_send.at[i],
            recv_sem=col_recv.at[i], device_id=at(i, 0), device_id_type=MESH,
        )

    def start_row(i, carry):
        row_copy(i).start()
        return carry

    def start_col(i, carry):
        col_copy(i).start()
        return carry

    def wait_row(i, carry):
        row_copy(i).wait_recv()
        return carry

    def wait_col(i, carry):
        col_copy(i).wait_recv()
        return carry

    lax.fori_loop(1, n_grp, start_row, 0)
    copies = []

    def push(source, target, blocks, step_cols, step_grp):
        i = len(copies)
        copy = pltpu.make_async_remote_copy(
            src_ref=blk.at[pl.ds(source, blocks)], dst_ref=blk.at[pl.ds(target, blocks)],
            send_sem=send_sem.at[i], recv_sem=recv_sem.at[i],
            device_id=at(step_cols, step_grp), device_id_type=MESH,
        )
        copy.start()
        copies.append(copy)
        return copy

    def pick(at_even, at_odd):
        return at_even + (at_odd - at_even) * odd

    centre = push(4, pick(straight[1] + 1, straight[-1] + 1), 1, -side, 0)
    opposite = push(4, pick(straight[-1] + 1, straight[1] + 1), 1, side, 0)
    shared = push(pick(5, 3), pick(straight[1] + 2, straight[-1]), 1, -side, 0)
    push(pick(3, 5), pick(straight[1], straight[-1] + 2), 1, -side, 0)
    push(pick(3, 5), pick(straight[-1], straight[1] + 2), 1, side, 0)
    for offset, first, blocks, slot in placed:
        if offset[0] == 0:
            push(first, slot, blocks, 0, -offset[1])

    lax.fori_loop(1, n_grp, wait_row, 0)
    col_sums[0] = jnp.sum(row_sums[...], axis=0)
    lax.fori_loop(1, n_cols, start_col, 0)

    count = cnt[0, 0]
    ids = [nbr[0, 0, p] for p in range(SLOTS)]

    def put(p, q, value):
        top = value.astype(jnp.bfloat16)
        rows, columns = pl.ds(p * width, width), pl.ds(q * width, width)
        high[rows, columns] = top
        low[rows, columns] = (value - top.astype(jnp.float32)).astype(jnp.bfloat16)

    centre.wait_recv()
    held = pick(straight[1] + 1, straight[-1] + 1)
    push(held, pick(corner[1, 1], corner[-1, -1]), 1, 0, -side)
    push(held, pick(corner[1, -1], corner[-1, 1]), 1, 0, side)
    opposite.wait_recv()
    held = pick(straight[-1] + 1, straight[1] + 1)
    push(held, pick(corner[-1, 1], corner[1, -1]), 1, 0, -side)
    push(held, pick(corner[-1, -1], corner[1, 1]), 1, 0, side)
    shared.wait_recv()
    push(pick(straight[1] + 2, straight[-1]), pick(straight[1], straight[-1] + 2), 1, 0, side)
    relayed = (centre, opposite, shared)
    for copy in copies:
        if all(copy is not done for done in relayed):
            copy.wait_recv()

    for p in range(SLOTS):
        for q in range(p + 1):
            code = table[ids[p] * STENCIL + ids[q]]
            usable = (code < MISSING) & (p < count)
            turned = (code >= TURNED) & (code < MISSING)
            slot = lax.rem(code, TURNED)
            block = blk[slot]
            block = jnp.where(usable, block, 0.0)
            if p == q:
                put(p, q, block)
            else:
                other = block.T
                put(p, q, jnp.where(turned, other, block))
                put(q, p, jnp.where(turned, block, other))

    lax.fori_loop(1, n_cols, wait_col, 0)
    sum_squares = jnp.sum(jnp.sum(col_sums[...], axis=0), keepdims=True)
    rows_total = width * n_cols * n_grp
    inverse = 0.5 * lax.rsqrt(sum_squares / rows_total + 1e-06)

    def times(vector):
        top = vector.astype(jnp.bfloat16)
        rest = (vector - top.astype(jnp.float32)).astype(jnp.bfloat16)
        both = jnp.concatenate([top, rest], axis=1)
        main = jnp.dot(high[...], both, preferred_element_type=jnp.float32)
        side = jnp.dot(low[...], top, preferred_element_type=jnp.float32)
        return (main[:, :width] + (main[:, width:] + side)) * inverse

    first = high[:, pl.ds(0, width)].astype(jnp.float32) + low[:, pl.ds(0, width)].astype(jnp.float32)
    initial = first * inverse
    column = 1.5 * initial - 0.5 * times(times(initial))
    image = column
    for _ in range(2):
        once = times(image)
        image = 1.5 * once - 0.5 * times(times(once))
    sign = 1.5 * column - 0.5 * image
    diagonal = lax.broadcasted_iota(jnp.int32, sign.shape, 0) == lax.broadcasted_iota(
        jnp.int32, sign.shape, 1
    )
    dens[...] = (0.5 * (jnp.where(diagonal, 1.0, 0.0) - sign)).reshape(dens.shape)

    for k in range(STENCIL):
        place, named = jnp.int32(0), jnp.int32(0)
        for p in range(SLOTS):
            hit = ((ids[p] == k) & (p < count)).astype(jnp.int32)
            place, named = place + p * hit, named + hit
        out[0, 0, k] = jnp.where(named > 0, dens[place], 0.0)

    def done_row(i, carry):
        row_copy(i).wait_send()
        return carry

    def done_col(i, carry):
        col_copy(i).wait_send()
        return carry

    for copy in copies:
        copy.wait_send()
    lax.fori_loop(1, n_grp, done_row, 0)
    lax.fori_loop(1, n_cols, done_col, 0)


def shards(hcols, neighbours, counts, n_cols, n_grp):
    width = hcols.shape[-1]
    placed, slots = transfers()
    order = SLOTS * width
    dma = pltpu.SemaphoreType.DMA
    hcols, neighbours = (
        pltpu.with_memory_space_constraint(each, pltpu.HBM) for each in (hcols, neighbours)
    )
    return pl.pallas_call(
        functools.partial(kernel, n_cols, n_grp),
        out_shape=jax.ShapeDtypeStruct(hcols.shape, jnp.float32),
        in_specs=[
            pl.BlockSpec(memory_space=pltpu.HBM),
            pl.BlockSpec(memory_space=pltpu.HBM),
            pl.BlockSpec(memory_space=pltpu.HBM),
        ],
        out_specs=pl.BlockSpec(memory_space=pltpu.VMEM),
        scratch_shapes=[
            pltpu.SMEM(neighbours.shape, jnp.int32),
            pltpu.SMEM(counts.shape, jnp.int32),
            pltpu.VMEM((slots, width, width), jnp.float32),
            pltpu.SMEM((STENCIL * STENCIL,), jnp.int32),
            pltpu.VMEM((order, order), jnp.bfloat16),
            pltpu.VMEM((order, order), jnp.bfloat16),
            pltpu.VMEM((SLOTS, width, width), jnp.float32),
            pltpu.VMEM((n_grp, 8, width), jnp.float32),
            pltpu.VMEM((n_cols, 8, width), jnp.float32),
            dma((2,)),
            dma,
            dma((len(placed) + 4,)),
            dma((len(placed) + 4,)),
            dma((n_grp,)),
            dma((n_grp,)),
            dma((n_cols,)),
            dma((n_cols,)),
        ],
        compiler_params=pltpu.CompilerParams(
            collective_id=0, has_side_effects=True, vmem_limit_bytes=24 * 1024 * 1024
        ),
        name="density_columns",
    )(hcols, neighbours, counts)


def solution(mesh):
    in_specs = (P("cols", "grp", None, None, None), P("cols", "grp", None), P("cols", "grp"))
    out_specs = P("cols", "grp", None, None, None)
    body = functools.partial(shards, n_cols=mesh.shape["cols"], n_grp=mesh.shape["grp"])
    return jax.shard_map(body, mesh=mesh, in_specs=in_specs, out_specs=out_specs, check_vma=False)
```
